1024 devices in a mesh: row: 16 (over x, z_hi), col: 64 (over y, z_lo, core).
Axes of the slice: x: 4, y: 4, z: 32 (z_hi: 4, z_lo: 8; z = z_hi * 8 + z_lo), core: 2. Of those that a mesh axis runs over, the one named last changes fastest.
Arguments:
- iterate: bfloat16 [4096, 6144], P(('row', 'col')), may hold values from -0.25 to 0.25
Outputs:
- update: bfloat16 [4096, 6144], P('row', 'col')
The draws below stay inside these ranges and needn't reach their ends.
All inputs are finite; a program needn't handle non-finite values.
Results may differ from the reference program's by a relative error of at most 0.0084.
Values may be sent and summed in bfloat16 or wider, within the bound.
A program may use at most 32 MiB of HBM per device.

```python
import math
import jax
import jax.numpy as jnp
from jax import lax

M = 4096
D = 6144


def draw_iterate(key, part):
    folded = jax.random.fold_in(key, 17)
    key_base, key_rows, key_cols = jax.random.split(folded, 3)
    spread_log = math.log(2.0)
    base_field = jnp.clip(jax.random.normal(key_base, (M, D), jnp.float32), -6.0, 6.0)
    row_scale = jnp.exp(jax.random.uniform(key_rows, (M, 1), jnp.float32, 0.0, spread_log))
    col_scale = jnp.exp(jax.random.uniform(key_cols, (1, D), jnp.float32, 0.0, spread_log))
    mean_square = (math.exp(2.0 * spread_log) - 1.0) / (2.0 * spread_log)
    factor = 0.6 / (math.sqrt(D) * mean_square)
    return (factor * base_field * row_scale * col_scale).astype(jnp.bfloat16)


def setup_inputs(seed: int = 0) -> dict:
    arg_keys = jax.random.split(jax.random.key(seed), 2)
    return {
        "iterate": draw_iterate(jax.random.fold_in(arg_keys[1], 71), 0),
    }


linear_weight = 3.4445
cubic_weight = -4.775
quintic_weight = 2.0315
output_gain = 0.2

def reference(iterate):
    gram_matrix = lax.dot_general(iterate, iterate, (((1,), (1,)), ((), ())), preferred_element_type=jnp.float32).astype(jnp.bfloat16)
    image_matrix = jnp.dot(gram_matrix, iterate, preferred_element_type=jnp.float32).astype(jnp.bfloat16)
    second_term = jnp.dot(gram_matrix, image_matrix, preferred_element_type=jnp.float32)
    combined = linear_weight * iterate.astype(jnp.float32) + cubic_weight * image_matrix.astype(jnp.float32) + quintic_weight * second_term
    update = (output_gain * math.sqrt(max(M, D)) * combined).astype(jnp.bfloat16)
    return update
```

```python
import functools
import math

import jax
import jax.numpy as jnp
from jax import lax
from jax.experimental import pallas as pl
from jax.experimental.pallas import tpu as pltpu
from jax.sharding import PartitionSpec as P

M = 4096
D = 6144

linear_weight = 3.4445
cubic_weight = -4.775
quintic_weight = 2.0315
output_gain = 0.2

MESH = pl.DeviceIdType.MESH
ROWS = 64
WIDE = 384
STEPS = 16
PEERS = [(dx, dy) for dx in range(4) for dy in range(4)][1:]


def nt_dot(left, right):
    return lax.dot_general(
        left, right, (((1,), (1,)), ((), ())), preferred_element_type=jnp.float32
    )


def nn_dot(left, right):
    return jnp.dot(left, right, preferred_element_type=jnp.float32)


def await_bytes(ref, sem):
    pltpu.make_async_copy(ref, ref, sem).wait()


def kernel(
    x_ref,
    out_ref,
    pieces,
    tile32,
    xg,
    part,
    sums_in,
    wide,
    total,
    blocks,
    first_sem,
    ring_send,
    ring_recv,
    twin_send,
    twin_recv,
    rs_send,
    rs_recv,
    ag_send,
    ag_recv,
    last_send,
    last_recv,
):
    row = lax.axis_index("row")
    col = lax.axis_index("col")
    x, z_hi = row // 4, lax.rem(row, 4)
    y, z_lo, core = col // 16, lax.rem(col // 2, 8), lax.rem(col, 2)
    z = z_hi * 8 + z_lo

    def device(x_at, y_at, z_at, core_at):
        return (x_at * 4 + z_at // 8, y_at * 16 + lax.rem(z_at, 8) * 2 + core_at)

    def peer(dx, dy):
        return lax.rem(x + dx, 4), lax.rem(y + dy, 4)

    up = device(x, y, lax.rem(z + 1, 32), core)
    down = device(x, y, lax.rem(z + 31, 32), core)
    twin = (row, col + 1 - 2 * core)

    sends = []

    def push(src, dst, send_sem, recv_sem, target):
        copy = pltpu.make_async_remote_copy(
            src_ref=src,
            dst_ref=dst,
            send_sem=send_sem,
            recv_sem=recv_sem,
            device_id=target,
            device_id_type=MESH,
        )
        copy.start()
        return copy

    barrier = pltpu.get_barrier_semaphore()
    for dx, dy in PEERS:
        px, py = peer(dx, dy)
        pl.semaphore_signal(barrier, inc=1, device_id=device(px, py, z, core), device_id_type=MESH)
    for target in (up, down, twin):
        pl.semaphore_signal(barrier, inc=1, device_id=target, device_id_type=MESH)
    pl.semaphore_wait(barrier, 18)

    me = 4 * x + y
    for dx, dy in PEERS:
        px, py = peer(dx, dy)
        push(
            x_ref.at[4 * py + px],
            pieces.at[me],
            first_sem.at[0],
            first_sem.at[1],
            device(px, py, z, core),
        )
    pieces[me] = x_ref[4 * y + x]
    await_bytes(pieces.at[pl.ds(0, 15)], first_sem.at[1])
    for k in range(16):
        tile32[4 * k : 4 * k + 4, :] = pieces[k].astype(jnp.float32)
    last = 256 * 15
    xg[last : last + ROWS, :] = tile32[...].astype(jnp.bfloat16)
    await_bytes(pieces.at[pl.ds(0, 15)], first_sem.at[0])

    def slot(step, sign, mine):
        if step == 0:
            start = last
        elif step == STEPS:
            start = last + ROWS
        else:
            start = 256 * (step - 1) + (0 if sign > 0 else ROWS)
        return xg.at[pl.ds(start + (0 if mine else 2 * ROWS), ROWS), :]

    def sem_at(step, sign):
        return step if sign > 0 else STEPS + step

    def hop(step, sign):
        at = sem_at(step, sign)
        sends.append(
            push(
                slot(step - 1, sign, True),
                slot(step, sign, True),
                ring_send.at[at],
                ring_recv.at[at],
                up if sign > 0 else down,
            )
        )

    def share(step, sign):
        at = sem_at(step, sign)
        sends.append(
            push(
                slot(step, sign, True),
                slot(step, sign, False),
                twin_send.at[at],
                twin_recv.at[at],
                twin,
            )
        )

    tile = xg.at[pl.ds(last, ROWS), :]

    def partial(stage, left, group):
        b, g = group // 4, group % 4
        part[stage, b, :, 256 * g : 256 * g + 256] = nt_dot(
            left, xg[256 * group : 256 * group + 256, :]
        ).astype(jnp.bfloat16)

    def scatter(stage, b):
        for k, (dx, dy) in enumerate(PEERS):
            px, py = peer(dx, dy)
            push(
                part.at[
                    stage,
                    b,
                    pl.ds(pl.multiple_of(16 * px, 16), 16),
                    pl.ds(pl.multiple_of(256 * py, 256), 256),
                ],
                sums_in.at[stage, b, k],
                rs_send.at[stage, b],
                rs_recv.at[stage, b],
                device(px, py, z, core),
            )

    def spread(stage, b):
        await_bytes(sums_in.at[stage, b], rs_recv.at[stage, b])
        rows = pl.ds(pl.multiple_of(16 * x, 16), 16)
        columns = pl.ds(pl.multiple_of(256 * y, 256), 256)
        acc = part[stage, b, rows, columns].astype(jnp.float32)
        for k in range(15):
            acc += sums_in[stage, b, k].astype(jnp.float32)
        wide[stage, b, rows, columns] = acc.astype(jnp.bfloat16)
        for dx, dy in PEERS:
            px, py = peer(dx, dy)
            push(
                wide.at[stage, b, rows, columns],
                wide.at[stage, b, rows, columns],
                ag_send.at[stage, b],
                ag_recv.at[stage, b],
                device(px, py, z, core),
            )

    def accumulate(stage, b):
        await_bytes(sums_in.at[stage, b], ag_recv.at[stage, b])
        product = nn_dot(wide[stage, b], xg[1024 * b : 1024 * b + 1024, :])
        if b == 0:
            total[stage] = product
        else:
            total[stage] += product

    share(0, 1)
    hop(1, 1)
    hop(1, -1)

    def ready(step):
        for sign in (1, -1):
            if step == STEPS and sign < 0:
                continue
            at = sem_at(step, sign)
            await_bytes(slot(step, sign, False), twin_recv.at[at])

    todo = {
        5: lambda: scatter(0, 0),
        9: lambda: (spread(0, 0), scatter(0, 1)),
        13: lambda: (accumulate(0, 0), spread(0, 1), scatter(0, 2)),
        16: lambda: (accumulate(0, 1),),
    }
    for step in range(1, STEPS + 1):
        for sign in (1, -1):
            if step == STEPS and sign < 0:
                continue
            await_bytes(slot(step, sign, True), ring_recv.at[sem_at(step, sign)])
            if step < STEPS and not (step == STEPS - 1 and sign < 0):
                hop(step + 1, sign)
        for sign in (1, -1):
            if not (step == STEPS and sign < 0):
                share(step, sign)
        if step > 1:
            ready(step - 1)
            partial(0, tile[...], step - 2)
        if step in todo:
            todo[step]()
    await_bytes(slot(0, 1, False), twin_recv.at[0])
    ready(STEPS)
    partial(0, tile[...], 15)
    scatter(0, 3)
    spread(0, 2)
    accumulate(0, 2)
    spread(0, 3)
    accumulate(0, 3)

    image = total[0].astype(jnp.bfloat16)
    for b in range(4):
        for g in range(4):
            partial(1, image, 4 * b + g)
        scatter(1, b)
    for b in range(4):
        spread(1, b)
    for b in range(4):
        accumulate(1, b)

    update = (output_gain * math.sqrt(max(M, D))) * (
        linear_weight * tile[...].astype(jnp.float32)
        + cubic_weight * image.astype(jnp.float32)
        + quintic_weight * total[1]
    )
    update = jnp.concatenate([update, jnp.zeros((ROWS, 128), jnp.float32)], axis=1)
    for j in range(4):
        block = update[:, 96 * j : 96 * j + 128].astype(jnp.bfloat16)
        for k in range(4):
            blocks[k, j] = block[16 * k : 16 * k + 16, :]

    landing = z_lo * 2 + core
    first_col = 16 * y + 4 * x

    def last_copy(k, j):
        return pltpu.make_async_remote_copy(
            src_ref=blocks.at[k, j],
            dst_ref=out_ref.at[landing],
            send_sem=last_send.at[4 * k + j],
            recv_sem=last_recv.at[landing],
            device_id=(4 * k + z_hi, first_col + j),
            device_id_type=MESH,
        )

    for k in range(4):
        for j in range(4):
            away = jnp.logical_or(x != k, col != first_col + j)

            @pl.when(away)
            def _(k=k, j=j):
                last_copy(k, j).start()

            @pl.when(jnp.logical_not(away))
            def _(k=k, j=j):
                pltpu.make_async_copy(
                    blocks.at[k, j], out_ref.at[landing], last_recv.at[landing]
                ).start()

    for copy in sends:
        copy.wait_send()
    for stage in range(2):
        for b in range(4):
            await_bytes(sums_in.at[stage, b], rs_send.at[stage, b])
            await_bytes(sums_in.at[stage, b], ag_send.at[stage, b])
    for k in range(16):
        await_bytes(out_ref.at[k], last_recv.at[k])
    for k in range(4):
        for j in range(4):

            @pl.when(jnp.logical_or(x != k, col != first_col + j))
            def _(k=k, j=j):
                last_copy(k, j).wait_send()


def shards(iterate):
    pieces = jnp.transpose(iterate.reshape(4, 16, WIDE), (1, 0, 2))
    spec = pl.BlockSpec(memory_space=pltpu.VMEM)
    landed = pl.pallas_call(
        kernel,
        out_shape=jax.ShapeDtypeStruct((16, 16, 128), jnp.bfloat16),
        in_specs=[spec],
        out_specs=spec,
        scratch_shapes=[
            pltpu.VMEM((16, 4, WIDE), jnp.bfloat16),
            pltpu.VMEM((ROWS, WIDE), jnp.float32),
            pltpu.VMEM((M, WIDE), jnp.bfloat16),
            pltpu.VMEM((2, 4, ROWS, 1024), jnp.bfloat16),
            pltpu.VMEM((2, 4, 15, 16, 256), jnp.bfloat16),
            pltpu.VMEM((2, 4, ROWS, 1024), jnp.bfloat16),
            pltpu.VMEM((2, ROWS, WIDE), jnp.float32),
            pltpu.VMEM((4, 4, 16, 128), jnp.bfloat16),
            pltpu.SemaphoreType.DMA((2,)),
            pltpu.SemaphoreType.DMA((32,)),
            pltpu.SemaphoreType.DMA((32,)),
            pltpu.SemaphoreType.DMA((32,)),
            pltpu.SemaphoreType.DMA((32,)),
            pltpu.SemaphoreType.DMA((2, 4)),
            pltpu.SemaphoreType.DMA((2, 4)),
            pltpu.SemaphoreType.DMA((2, 4)),
            pltpu.SemaphoreType.DMA((2, 4)),
            pltpu.SemaphoreType.DMA((16,)),
            pltpu.SemaphoreType.DMA((16,)),
        ],
        compiler_params=pltpu.CompilerParams(collective_id=0, has_side_effects=True),
    )(pieces)
    tiles = landed.reshape(16, 4, 4, 128)[..., :96]
    return jnp.transpose(tiles, (1, 0, 2, 3)).reshape(256, 96)


def solution(mesh):
    return jax.shard_map(
        shards,
        mesh=mesh,
        in_specs=(P(("row", "col"), None),),
        out_specs=P("row", "col"),
        check_vma=False,
    )
```

```python
import functools
import math

import jax
import jax.numpy as jnp
from jax import lax
from jax.experimental import pallas as pl
from jax.experimental.pallas import tpu as pltpu
from jax.sharding import PartitionSpec as P

M = 4096
D = 6144

linear_weight = 3.4445
cubic_weight = -4.775
quintic_weight = 2.0315
output_gain = 0.2

MESH = pl.DeviceIdType.MESH
ROWS = 64
WIDE = 384
STEPS = 16
STRIDE = 3


def taken_from():
    source = {}
    for far in range(1, STEPS + 1):
        stop = (2 * far + STRIDE) // (2 * STRIDE) * STRIDE
        stop -= STRIDE if stop >= STEPS else 0
        source[far] = far - STRIDE if far == stop else far - 1 if far > stop else far + 1
    return source


SOURCE = taken_from()
CHILDREN = {
    far: sorted((c for c in SOURCE if SOURCE[c] == far), key=lambda c: -abs(c - far))
    for far in range(STEPS + 1)
}


def arrival(far):
    return 0.0 if far == 0 else arrival(SOURCE[far]) + 3.3 + 0.8 * abs(far - SOURCE[far])


ORDER = sorted(range(1, STEPS + 1), key=lambda far: (arrival(far), far))
REACH = sorted({s * (c - SOURCE[c]) for c in SOURCE for s in (1, -1)})
PEERS = sorted(
    [(dx, dy) for dx in range(4) for dy in range(4)][1:],
    key=lambda d: -min(d[0], 4 - d[0]) - min(d[1], 4 - d[1]),
)


def nt_dot(left, right):
    return lax.dot_general(
        left, right, (((1,), (1,)), ((), ())), preferred_element_type=jnp.float32
    )


def nn_dot(left, right):
    return jnp.dot(left, right, preferred_element_type=jnp.float32)


def await_bytes(ref, sem):
    pltpu.make_async_copy(ref, ref, sem).wait()


def kernel(
    x_ref,
    out_ref,
    pieces,
    tile32,
    xg,
    part,
    sums_in,
    wide,
    total,
    blocks,
    landed,
    out32,
    first_sem,
    ring_send,
    ring_recv,
    twin_send,
    twin_recv,
    rs_send,
    rs_recv,
    ag_send,
    ag_recv,
    last_send,
    last_recv,
):
    row = lax.axis_index("row")
    col = lax.axis_index("col")
    x, z_hi = row // 4, lax.rem(row, 4)
    y, z_lo, core = col // 16, lax.rem(col // 2, 8), lax.rem(col, 2)
    z = z_hi * 8 + z_lo

    def device(x_at, y_at, z_at, core_at):
        return (x_at * 4 + z_at // 8, y_at * 16 + lax.rem(z_at, 8) * 2 + core_at)

    def peer(dx, dy):
        return lax.rem(x + dx, 4), lax.rem(y + dy, 4)

    def column(far):
        return lax.rem(z + 32 + far, 32)

    twin = device(x, y, z, 1 - core)

    sends = []

    def push(src, dst, send_sem, recv_sem, target):
        copy = pltpu.make_async_remote_copy(
            src_ref=src,
            dst_ref=dst,
            send_sem=send_sem,
            recv_sem=recv_sem,
            device_id=target,
            device_id_type=MESH,
        )
        copy.start()
        return copy

    barrier = pltpu.get_barrier_semaphore()
    for dx, dy in PEERS:
        px, py = peer(dx, dy)
        pl.semaphore_signal(barrier, inc=1, device_id=device(px, py, z, core), device_id_type=MESH)
    greeted = [(x, y, column(far), core) for far in REACH]
    greeted.append((x, y, z, 1 - core))
    for target in greeted:
        pl.semaphore_signal(barrier, inc=1, device_id=device(*target), device_id_type=MESH)
    pl.semaphore_wait(barrier, 15 + len(greeted))

    me = 4 * x + y
    for dx, dy in PEERS:
        px, py = peer(dx, dy)
        push(
            x_ref.at[4 * py + px],
            pieces.at[me],
            first_sem.at[0],
            first_sem.at[1],
            device(px, py, z, core),
        )
    pieces[me] = x_ref[4 * y + x]
    await_bytes(pieces.at[pl.ds(0, 15)], first_sem.at[1])
    for k in range(16):
        tile32[4 * k : 4 * k + 4, :] = pieces[k].astype(jnp.float32)
    last = 256 * 15
    xg[last : last + ROWS, :] = tile32[...].astype(jnp.bfloat16)

    def slot(far, sign, mine):
        if far == 0:
            start = last
        elif far == STEPS:
            start = last + ROWS
        else:
            start = 256 * ORDER.index(far) + (0 if sign > 0 else ROWS)
        return xg.at[pl.ds(start + (0 if mine else 2 * ROWS), ROWS), :]

    def sem_at(far, sign):
        return far if sign > 0 else STEPS + far

    def signs(far):
        return (1,) if far in (0, STEPS) else (1, -1)

    def hand_on(far):
        for child in CHILDREN[far]:
            for sign in (1, -1):
                if child == STEPS and sign < 0:
                    continue
                at = sem_at(child, sign)
                target = column(sign * (child - far))
                sends.append(
                    push(
                        slot(far, sign, True),
                        slot(child, sign, True),
                        ring_send.at[at],
                        ring_recv.at[at],
                        device(x, y, target, core),
                    )
                )

    def share(far):
        for sign in signs(far):
            at = sem_at(far, sign)
            sends.append(
                push(
                    slot(far, sign, True),
                    slot(far, sign, False),
                    twin_send.at[at],
                    twin_recv.at[at],
                    twin,
                )
            )

    def shared(far):
        for sign in signs(far):
            await_bytes(slot(far, sign, False), twin_recv.at[sem_at(far, sign)])

    tile = xg.at[pl.ds(last, ROWS), :]

    def partial(stage, left, group):
        b, g = group // 4, group % 4
        part[stage, b, :, 256 * g : 256 * g + 256] = nt_dot(
            left, xg[256 * group : 256 * group + 256, :]
        ).astype(jnp.bfloat16)

    def scatter(stage, b):
        for k, (dx, dy) in enumerate(PEERS):
            px, py = peer(dx, dy)
            push(
                part.at[
                    stage,
                    b,
                    pl.ds(pl.multiple_of(16 * px, 16), 16),
                    pl.ds(pl.multiple_of(256 * py, 256), 256),
                ],
                sums_in.at[stage, b, k],
                rs_send.at[stage, b],
                rs_recv.at[stage, b],
                device(px, py, z, core),
            )

    def spread(stage, b):
        await_bytes(sums_in.at[stage, b], rs_recv.at[stage, b])
        rows = pl.ds(pl.multiple_of(16 * x, 16), 16)
        columns = pl.ds(pl.multiple_of(256 * y, 256), 256)
        acc = part[stage, b, rows, columns].astype(jnp.float32)
        for k in range(15):
            acc += sums_in[stage, b, k].astype(jnp.float32)
        wide[stage, b, rows, columns] = acc.astype(jnp.bfloat16)
        for dx, dy in PEERS:
            px, py = peer(dx, dy)
            push(
                wide.at[stage, b, rows, columns],
                wide.at[stage, b, rows, columns],
                ag_send.at[stage, b],
                ag_recv.at[stage, b],
                device(px, py, z, core),
            )

    def accumulate(stage, b):
        await_bytes(sums_in.at[stage, b], ag_recv.at[stage, b])
        product = nn_dot(wide[stage, b], xg[1024 * b : 1024 * b + 1024, :])
        if b == 0:
            total[stage] = product
        else:
            total[stage] += product

    hand_on(0)
    share(0)
    groups, spreads, sums = list(range(15)), [], []
    for far in ORDER:
        now = arrival(far)
        for sign in signs(far):
            await_bytes(slot(far, sign, True), ring_recv.at[sem_at(far, sign)])
        hand_on(far)
        share(far)
        while groups and arrival(ORDER[groups[0]]) + 4.0 <= now:
            group = groups.pop(0)
            shared(ORDER[group])
            partial(0, tile[...], group)
            if group % 4 == 3:
                scatter(0, group // 4)
                spreads.append((now + 8.0, group // 4))
        while spreads and spreads[0][0] <= now:
            b = spreads.pop(0)[1]
            spread(0, b)
            sums.append((now + 8.0, b))
        while sums and sums[0][0] <= now:
            accumulate(0, sums.pop(0)[1])
    for group in groups + [15]:
        if group < 15:
            shared(ORDER[group])
        else:
            shared(STEPS)
            shared(0)
        partial(0, tile[...], group)
        if group % 4 == 3:
            scatter(0, group // 4)
            spreads.append((0.0, group // 4))
    for _, b in spreads[:-1]:
        spread(0, b)
        sums.append((0.0, b))
    for _, b in sums[:-1]:
        accumulate(0, b)
    spread(0, 3)
    accumulate(0, sums[-1][1])
    accumulate(0, 3)

    image = total[0].astype(jnp.bfloat16)
    for b in range(4):
        for g in range(4):
            partial(1, image, 4 * b + g)
        scatter(1, b)
    for b in range(4):
        spread(1, b)
    for b in range(4):
        accumulate(1, b)

    update = (output_gain * math.sqrt(max(M, D))) * (
        linear_weight * tile[...].astype(jnp.float32)
        + cubic_weight * image.astype(jnp.float32)
        + quintic_weight * total[1]
    )
    update = jnp.concatenate([update, jnp.zeros((ROWS, 128), jnp.float32)], axis=1)
    for j in range(4):
        block = update[:, 96 * j : 96 * j + 128].astype(jnp.bfloat16)
        for k in range(4):
            blocks[k, j] = block[16 * k : 16 * k + 16, :]

    landing = z_lo * 2 + core
    first_col = 16 * y + 4 * x

    def last_copy(k, j):
        return pltpu.make_async_remote_copy(
            src_ref=blocks.at[k, j],
            dst_ref=landed.at[landing],
            send_sem=last_send.at[4 * k + j],
            recv_sem=last_recv.at[landing],
            device_id=(4 * k + z_hi, first_col + j),
            device_id_type=MESH,
        )

    for k in range(4):
        for j in range(4):
            away = jnp.logical_or(x != k, col != first_col + j)

            @pl.when(away)
            def _(k=k, j=j):
                last_copy(k, j).start()

            @pl.when(jnp.logical_not(away))
            def _(k=k, j=j):
                pltpu.make_async_copy(
                    blocks.at[k, j], landed.at[landing], last_recv.at[landing]
                ).start()

    for k in range(16):
        await_bytes(landed.at[k], last_recv.at[k])
        block = landed[k].astype(jnp.float32)
        for j in range(4):
            out32[64 * j + 4 * k : 64 * j + 4 * k + 4, :] = block[4 * j : 4 * j + 4, :]
    out_ref[...] = out32[:, :96].astype(jnp.bfloat16)
    await_bytes(pieces.at[pl.ds(0, 15)], first_sem.at[0])
    for copy in sends:
        copy.wait_send()
    for stage in range(2):
        for b in range(4):
            await_bytes(sums_in.at[stage, b], rs_send.at[stage, b])
            await_bytes(sums_in.at[stage, b], ag_send.at[stage, b])
    for k in range(4):
        for j in range(4):

            @pl.when(jnp.logical_or(x != k, col != first_col + j))
            def _(k=k, j=j):
                last_copy(k, j).wait_send()


def shards(iterate):
    pieces = jnp.transpose(iterate.reshape(4, 16, WIDE), (1, 0, 2))
    spec = pl.BlockSpec(memory_space=pltpu.VMEM)
    return pl.pallas_call(
        kernel,
        out_shape=jax.ShapeDtypeStruct((256, 96), jnp.bfloat16),
        in_specs=[spec],
        out_specs=spec,
        scratch_shapes=[
            pltpu.VMEM((16, 4, WIDE), jnp.bfloat16),
            pltpu.VMEM((ROWS, WIDE), jnp.float32),
            pltpu.VMEM((M, WIDE), jnp.bfloat16),
            pltpu.VMEM((2, 4, ROWS, 1024), jnp.bfloat16),
            pltpu.VMEM((2, 4, 15, 16, 256), jnp.bfloat16),
            pltpu.VMEM((2, 4, ROWS, 1024), jnp.bfloat16),
            pltpu.VMEM((2, ROWS, WIDE), jnp.float32),
            pltpu.VMEM((4, 4, 16, 128), jnp.bfloat16),
            pltpu.VMEM((16, 16, 128), jnp.bfloat16),
            pltpu.VMEM((256, 128), jnp.float32),
            pltpu.SemaphoreType.DMA((2,)),
            pltpu.SemaphoreType.DMA((32,)),
            pltpu.SemaphoreType.DMA((32,)),
            pltpu.SemaphoreType.DMA((32,)),
            pltpu.SemaphoreType.DMA((32,)),
            pltpu.SemaphoreType.DMA((2, 4)),
            pltpu.SemaphoreType.DMA((2, 4)),
            pltpu.SemaphoreType.DMA((2, 4)),
            pltpu.SemaphoreType.DMA((2, 4)),
            pltpu.SemaphoreType.DMA((16,)),
            pltpu.SemaphoreType.DMA((16,)),
        ],
        compiler_params=pltpu.CompilerParams(collective_id=0, has_side_effects=True),
    )(pieces)


def solution(mesh):
    return jax.shard_map(
        shards,
        mesh=mesh,
        in_specs=(P(("row", "col"), None),),
        out_specs=P("row", "col"),
        check_vma=False,
    )
```

```python
import functools
import math

import jax
import jax.numpy as jnp
from jax import lax
from jax.experimental import pallas as pl
from jax.experimental.pallas import tpu as pltpu
from jax.sharding import PartitionSpec as P

M = 4096
D = 6144

linear_weight = 3.4445
cubic_weight = -4.775
quintic_weight = 2.0315
output_gain = 0.2

MESH = pl.DeviceIdType.MESH
ROWS = 64
WIDE = 384
STEPS = 16
STRIDE = 3
PARTS = 2
PIECE = ROWS // PARTS


def taken_from():
    source = {}
    for far in range(1, STEPS + 1):
        stop = (2 * far + STRIDE) // (2 * STRIDE) * STRIDE
        stop -= STRIDE if stop >= STEPS else 0
        source[far] = far - STRIDE if far == stop else far - 1 if far > stop else far + 1
    return source


SOURCE = taken_from()
CHILDREN = {
    far: sorted((c for c in SOURCE if SOURCE[c] == far), key=lambda c: -abs(c - far))
    for far in range(STEPS + 1)
}


def arrival(far):
    if far == 0:
        return 0.0
    hops = abs(far - SOURCE[far])
    return arrival(SOURCE[far]) + 3.3 + 0.8 * hops + (6.0 if hops == 1 else 0.0)


ORDER = sorted(range(1, STEPS + 1), key=lambda far: (arrival(far), far))
REACH = sorted({s * (c - SOURCE[c]) for c in SOURCE for s in (1, -1)})
PEERS = sorted(
    [(dx, dy) for dx in range(4) for dy in range(4)][1:],
    key=lambda d: -min(d[0], 4 - d[0]) - min(d[1], 4 - d[1]),
)


def nt_dot(left, right):
    return lax.dot_general(
        left, right, (((1,), (1,)), ((), ())), preferred_element_type=jnp.float32
    )


def nn_dot(left, right):
    return jnp.dot(left, right, preferred_element_type=jnp.float32)


def await_bytes(ref, sem):
    pltpu.make_async_copy(ref, ref, sem).wait()


def kernel(
    x_ref,
    out_ref,
    pieces,
    tile32,
    xg,
    part,
    sums_in,
    wide,
    total,
    blocks,
    landed,
    out32,
    first_sem,
    ring_send,
    ring_recv,
    twin_send,
    twin_recv,
    rs_send,
    rs_recv,
    ag_send,
    ag_recv,
    last_send,
    last_recv,
):
    row = lax.axis_index("row")
    col = lax.axis_index("col")
    x, z_hi = row // 4, lax.rem(row, 4)
    y, z_lo, core = col // 16, lax.rem(col // 2, 8), lax.rem(col, 2)
    z = z_hi * 8 + z_lo

    def device(x_at, y_at, z_at, core_at):
        return (x_at * 4 + z_at // 8, y_at * 16 + lax.rem(z_at, 8) * 2 + core_at)

    def peer(dx, dy):
        return lax.rem(x + dx, 4), lax.rem(y + dy, 4)

    def column(far):
        return lax.rem(z + 32 + far, 32)

    twin = device(x, y, z, 1 - core)

    sends = []

    def push(src, dst, send_sem, recv_sem, target):
        copy = pltpu.make_async_remote_copy(
            src_ref=src,
            dst_ref=dst,
            send_sem=send_sem,
            recv_sem=recv_sem,
            device_id=target,
            device_id_type=MESH,
        )
        copy.start()
        return copy

    barrier = pltpu.get_barrier_semaphore()
    for dx, dy in PEERS:
        px, py = peer(dx, dy)
        pl.semaphore_signal(barrier, inc=1, device_id=device(px, py, z, core), device_id_type=MESH)
    greeted = [(x, y, column(far), core) for far in REACH]
    greeted.append((x, y, z, 1 - core))
    for target in greeted:
        pl.semaphore_signal(barrier, inc=1, device_id=device(*target), device_id_type=MESH)
    pl.semaphore_wait(barrier, 15 + len(greeted))

    me = 4 * x + y
    for dx, dy in PEERS:
        px, py = peer(dx, dy)
        push(
            x_ref.at[4 * py + px],
            pieces.at[me],
            first_sem.at[0],
            first_sem.at[1],
            device(px, py, z, core),
        )
    pieces[me] = x_ref[4 * y + x]
    await_bytes(pieces.at[pl.ds(0, 15)], first_sem.at[1])
    for k in range(16):
        tile32[4 * k : 4 * k + 4, :] = pieces[k].astype(jnp.float32)
    last = 256 * 15
    xg[last : last + ROWS, :] = tile32[...].astype(jnp.bfloat16)

    def slot(far, sign, mine, part_of=None):
        if far == 0:
            start = last
        elif far == STEPS:
            start = last + ROWS
        else:
            start = 256 * ORDER.index(far) + (0 if sign > 0 else ROWS)
        start += 0 if mine else 2 * ROWS
        if part_of is None:
            return xg.at[pl.ds(start, ROWS), :]
        return xg.at[pl.ds(start + PIECE * part_of, PIECE), :]

    def sem_at(far, sign):
        return far if sign > 0 else STEPS + far

    def signs(far):
        return (1,) if far in (0, STEPS) else (1, -1)

    def hand_on(far, which, piece):
        for child in CHILDREN[far]:
            for sign in which:
                if child == STEPS and sign < 0:
                    continue
                at = sem_at(child, sign)
                sends.append(
                    push(
                        slot(far, sign, True, piece),
                        slot(child, sign, True, piece),
                        ring_send.at[piece, at],
                        ring_recv.at[piece, at],
                        device(x, y, column(sign * (child - far)), core),
                    )
                )

    def share(far):
        for sign in signs(far):
            at = sem_at(far, sign)
            sends.append(
                push(
                    slot(far, sign, True),
                    slot(far, sign, False),
                    twin_send.at[at],
                    twin_recv.at[at],
                    twin,
                )
            )

    def shared(far):
        for sign in signs(far):
            await_bytes(slot(far, sign, False), twin_recv.at[sem_at(far, sign)])

    tile = xg.at[pl.ds(last, ROWS), :]

    def partial(stage, left, group):
        b, g = group // 4, group % 4
        part[stage, b, :, 256 * g : 256 * g + 256] = nt_dot(
            left, xg[256 * group : 256 * group + 256, :]
        ).astype(jnp.bfloat16)

    def scatter(stage, b):
        for k, (dx, dy) in enumerate(PEERS):
            px, py = peer(dx, dy)
            push(
                part.at[
                    stage,
                    b,
                    pl.ds(pl.multiple_of(16 * px, 16), 16),
                    pl.ds(pl.multiple_of(256 * py, 256), 256),
                ],
                sums_in.at[stage, b, k],
                rs_send.at[stage, b],
                rs_recv.at[stage, b],
                device(px, py, z, core),
            )

    def spread(stage, b):
        await_bytes(sums_in.at[stage, b], rs_recv.at[stage, b])
        rows = pl.ds(pl.multiple_of(16 * x, 16), 16)
        columns = pl.ds(pl.multiple_of(256 * y, 256), 256)
        acc = part[stage, b, rows, columns].astype(jnp.float32)
        for k in range(15):
            acc += sums_in[stage, b, k].astype(jnp.float32)
        wide[stage, b, rows, columns] = acc.astype(jnp.bfloat16)
        for dx, dy in PEERS:
            px, py = peer(dx, dy)
            push(
                wide.at[stage, b, rows, columns],
                wide.at[stage, b, rows, columns],
                ag_send.at[stage, b],
                ag_recv.at[stage, b],
                device(px, py, z, core),
            )

    def accumulate(stage, b):
        await_bytes(sums_in.at[stage, b], ag_recv.at[stage, b])
        product = nn_dot(wide[stage, b], xg[1024 * b : 1024 * b + 1024, :])
        if b == 0:
            total[stage] = product
        else:
            total[stage] += product

    for piece in range(PARTS):
        hand_on(0, (1, -1), piece)
    share(0)
    groups, spreads, sums = list(range(15)), [], []
    for far in ORDER:
        now = arrival(far)
        for piece in range(PARTS):
            for sign in signs(far):
                await_bytes(slot(far, sign, True, piece), ring_recv.at[piece, sem_at(far, sign)])
                hand_on(far, (sign,), piece)
        share(far)
        while groups and arrival(ORDER[groups[0]]) + 4.0 <= now:
            group = groups.pop(0)
            shared(ORDER[group])
            partial(0, tile[...], group)
            if group % 4 == 3:
                scatter(0, group // 4)
                spreads.append((now + 8.0, group // 4))
        while spreads and spreads[0][0] <= now:
            b = spreads.pop(0)[1]
            spread(0, b)
            sums.append((now + 8.0, b))
        while sums and sums[0][0] <= now:
            accumulate(0, sums.pop(0)[1])
    for group in groups + [15]:
        if group < 15:
            shared(ORDER[group])
        else:
            shared(STEPS)
            shared(0)
        partial(0, tile[...], group)
        if group % 4 == 3:
            scatter(0, group // 4)
            spreads.append((0.0, group // 4))
    for _, b in spreads[:-1]:
        spread(0, b)
        sums.append((0.0, b))
    for _, b in sums[:-1]:
        accumulate(0, b)
    spread(0, 3)
    accumulate(0, sums[-1][1])
    accumulate(0, 3)

    image = total[0].astype(jnp.bfloat16)
    for b in range(4):
        for g in range(4):
            partial(1, image, 4 * b + g)
        scatter(1, b)
    for b in range(4):
        spread(1, b)
    for b in range(4):
        accumulate(1, b)

    update = (output_gain * math.sqrt(max(M, D))) * (
        linear_weight * tile[...].astype(jnp.float32)
        + cubic_weight * image.astype(jnp.float32)
        + quintic_weight * total[1]
    )
    update = jnp.concatenate([update, jnp.zeros((ROWS, 128), jnp.float32)], axis=1)
    for j in range(4):
        block = update[:, 96 * j : 96 * j + 128].astype(jnp.bfloat16)
        for k in range(4):
            blocks[k, j] = block[16 * k : 16 * k + 16, :]

    landing = z_lo * 2 + core
    first_col = 16 * y + 4 * x

    def last_copy(k, j):
        return pltpu.make_async_remote_copy(
            src_ref=blocks.at[k, j],
            dst_ref=landed.at[landing],
            send_sem=last_send.at[4 * k + j],
            recv_sem=last_recv.at[landing],
            device_id=(4 * k + z_hi, first_col + j),
            device_id_type=MESH,
        )

    for k in range(4):
        for j in range(4):
            away = jnp.logical_or(x != k, col != first_col + j)

            @pl.when(away)
            def _(k=k, j=j):
                last_copy(k, j).start()

            @pl.when(jnp.logical_not(away))
            def _(k=k, j=j):
                pltpu.make_async_copy(
                    blocks.at[k, j], landed.at[landing], last_recv.at[landing]
                ).start()

    for k in range(16):
        await_bytes(landed.at[k], last_recv.at[k])
        block = landed[k].astype(jnp.float32)
        for j in range(4):
            out32[64 * j + 4 * k : 64 * j + 4 * k + 4, :] = block[4 * j : 4 * j + 4, :]
    out_ref[...] = out32[:, :96].astype(jnp.bfloat16)
    await_bytes(pieces.at[pl.ds(0, 15)], first_sem.at[0])
    for copy in sends:
        copy.wait_send()
    for stage in range(2):
        for b in range(4):
            await_bytes(sums_in.at[stage, b], rs_send.at[stage, b])
            await_bytes(sums_in.at[stage, b], ag_send.at[stage, b])
    for k in range(4):
        for j in range(4):

            @pl.when(jnp.logical_or(x != k, col != first_col + j))
            def _(k=k, j=j):
                last_copy(k, j).wait_send()


def shards(iterate):
    pieces = jnp.transpose(iterate.reshape(4, 16, WIDE), (1, 0, 2))
    spec = pl.BlockSpec(memory_space=pltpu.VMEM)
    return pl.pallas_call(
        kernel,
        out_shape=jax.ShapeDtypeStruct((256, 96), jnp.bfloat16),
        in_specs=[spec],
        out_specs=spec,
        scratch_shapes=[
            pltpu.VMEM((16, 4, WIDE), jnp.bfloat16),
            pltpu.VMEM((ROWS, WIDE), jnp.float32),
            pltpu.VMEM((M, WIDE), jnp.bfloat16),
            pltpu.VMEM((2, 4, ROWS, 1024), jnp.bfloat16),
            pltpu.VMEM((2, 4, 15, 16, 256), jnp.bfloat16),
            pltpu.VMEM((2, 4, ROWS, 1024), jnp.bfloat16),
            pltpu.VMEM((2, ROWS, WIDE), jnp.float32),
            pltpu.VMEM((4, 4, 16, 128), jnp.bfloat16),
            pltpu.VMEM((16, 16, 128), jnp.bfloat16),
            pltpu.VMEM((256, 128), jnp.float32),
            pltpu.SemaphoreType.DMA((2,)),
            pltpu.SemaphoreType.DMA((PARTS, 32)),
            pltpu.SemaphoreType.DMA((PARTS, 32)),
            pltpu.SemaphoreType.DMA((32,)),
            pltpu.SemaphoreType.DMA((32,)),
            pltpu.SemaphoreType.DMA((2, 4)),
            pltpu.SemaphoreType.DMA((2, 4)),
            pltpu.SemaphoreType.DMA((2, 4)),
            pltpu.SemaphoreType.DMA((2, 4)),
            pltpu.SemaphoreType.DMA((16,)),
            pltpu.SemaphoreType.DMA((16,)),
        ],
        compiler_params=pltpu.CompilerParams(collective_id=0, has_side_effects=True),
    )(pieces)


def solution(mesh):
    return jax.shard_map(
        shards,
        mesh=mesh,
        in_specs=(P(("row", "col"), None),),
        out_specs=P("row", "col"),
        check_vma=False,
    )
```

```python
import functools
import math

import jax
import jax.numpy as jnp
from jax import lax
from jax.experimental import pallas as pl
from jax.experimental.pallas import tpu as pltpu
from jax.sharding import PartitionSpec as P

M = 4096
D = 6144

linear_weight = 3.4445
cubic_weight = -4.775
quintic_weight = 2.0315
output_gain = 0.2

MESH = pl.DeviceIdType.MESH
ROWS = 64
WIDE = 384
STEPS = 16
STRIDE = 3
LEAVES = (14, 16)
PARTS = 2
PIECE = ROWS // PARTS


def taken_from():
    source = {}
    for far in range(1, STEPS + 1):
        stop = (2 * far + STRIDE) // (2 * STRIDE) * STRIDE
        stop -= STRIDE if stop >= STEPS else 0
        source[far] = far - STRIDE if far == stop else far - 1 if far > stop else far + 1
    return source


SOURCE = taken_from()
CHILDREN = {
    far: sorted((c for c in SOURCE if SOURCE[c] == far), key=lambda c: -abs(c - far))
    for far in range(STEPS + 1)
}


def arrival(far):
    if far == 0:
        return 0.0
    hops = abs(far - SOURCE[far])
    return arrival(SOURCE[far]) + 3.3 + 0.8 * hops + (6.0 if hops == 1 else 0.0)


ORDER = sorted(range(1, STEPS + 1), key=lambda far: (arrival(far), far))
REACH = sorted({s * (c - SOURCE[c]) for c in SOURCE for s in (1, -1)})
PEERS = sorted(
    [(dx, dy) for dx in range(4) for dy in range(4)][1:],
    key=lambda d: -min(d[0], 4 - d[0]) - min(d[1], 4 - d[1]),
)


def nt_dot(left, right):
    return lax.dot_general(
        left, right, (((1,), (1,)), ((), ())), preferred_element_type=jnp.float32
    )


def nn_dot(left, right):
    return jnp.dot(left, right, preferred_element_type=jnp.float32)


def await_bytes(ref, sem):
    pltpu.make_async_copy(ref, ref, sem).wait()


def kernel(
    x_ref,
    out_ref,
    pieces,
    tile32,
    xg,
    part,
    sums_in,
    wide,
    total,
    blocks,
    landed,
    out32,
    first_sem,
    ring_send,
    ring_recv,
    twin_send,
    twin_recv,
    rs_send,
    rs_recv,
    ag_send,
    ag_recv,
    last_send,
    last_recv,
):
    row = lax.axis_index("row")
    col = lax.axis_index("col")
    x, z_hi = row // 4, lax.rem(row, 4)
    y, z_lo, core = col // 16, lax.rem(col // 2, 8), lax.rem(col, 2)
    z = z_hi * 8 + z_lo

    def device(x_at, y_at, z_at, core_at):
        return (x_at * 4 + z_at // 8, y_at * 16 + lax.rem(z_at, 8) * 2 + core_at)

    def peer(dx, dy):
        return lax.rem(x + dx, 4), lax.rem(y + dy, 4)

    def column(far):
        return lax.rem(z + 32 + far, 32)

    twin = device(x, y, z, 1 - core)

    sends = []

    def push(src, dst, send_sem, recv_sem, target):
        copy = pltpu.make_async_remote_copy(
            src_ref=src,
            dst_ref=dst,
            send_sem=send_sem,
            recv_sem=recv_sem,
            device_id=target,
            device_id_type=MESH,
        )
        copy.start()
        return copy

    barrier = pltpu.get_barrier_semaphore()
    for dx, dy in PEERS:
        px, py = peer(dx, dy)
        pl.semaphore_signal(barrier, inc=1, device_id=device(px, py, z, core), device_id_type=MESH)
    greeted = [(x, y, column(far), core) for far in REACH]
    greeted += [(x, y, column(far), 1 - core) for far in (1, 0, -1)]
    for target in greeted:
        pl.semaphore_signal(barrier, inc=1, device_id=device(*target), device_id_type=MESH)
    pl.semaphore_wait(barrier, 15 + len(greeted))

    me = 4 * x + y
    for dx, dy in PEERS:
        px, py = peer(dx, dy)
        push(
            x_ref.at[4 * py + px],
            pieces.at[me],
            first_sem.at[0],
            first_sem.at[1],
            device(px, py, z, core),
        )
    pieces[me] = x_ref[4 * y + x]
    await_bytes(pieces.at[pl.ds(0, 15)], first_sem.at[1])
    for k in range(16):
        tile32[4 * k : 4 * k + 4, :] = pieces[k].astype(jnp.float32)
    last = 256 * 15
    xg[last : last + ROWS, :] = tile32[...].astype(jnp.bfloat16)

    def slot(far, sign, mine, part_of=None):
        if far == 0:
            start = last
        elif far == STEPS:
            start = last + ROWS
        else:
            start = 256 * ORDER.index(far) + (0 if sign > 0 else ROWS)
        start += 0 if mine else 2 * ROWS
        if part_of is None:
            return xg.at[pl.ds(start, ROWS), :]
        return xg.at[pl.ds(start + PIECE * part_of, PIECE), :]

    def sem_at(far, sign):
        return far if sign > 0 or far == STEPS else STEPS + far

    def signs(far):
        return (1,) if far in (0, STEPS) else (1, -1)

    def hand_on(far, which, piece):
        for child in CHILDREN[far]:
            for sign in which:
                if child == STEPS and (sign > 0) != (piece < PARTS // 2):
                    continue
                at = sem_at(child, sign)
                sends.append(
                    push(
                        slot(far, sign, True, piece),
                        slot(child, sign, True, piece),
                        ring_send.at[piece, at],
                        ring_recv.at[piece, at],
                        device(x, y, column(sign * (child - far)), core),
                    )
                )
                if child in LEAVES:
                    sends.append(
                        push(
                            slot(far, sign, True, piece),
                            slot(child, sign, False, piece),
                            twin_send.at[piece, at],
                            twin_recv.at[piece, at],
                            device(x, y, column(sign * (child - far)), 1 - core),
                        )
                    )

    def share(far):
        for sign in signs(far):
            at = sem_at(far, sign)
            sends.append(
                push(
                    slot(far, sign, True),
                    slot(far, sign, False),
                    twin_send.at[0, at],
                    twin_recv.at[0, at],
                    twin,
                )
            )

    def shared(far):
        for sign in signs(far):
            at = sem_at(far, sign)
            if far in LEAVES:
                for piece in range(PARTS):
                    await_bytes(slot(far, sign, False, piece), twin_recv.at[piece, at])
            else:
                await_bytes(slot(far, sign, False), twin_recv.at[0, at])

    tile = xg.at[pl.ds(last, ROWS), :]

    def partial(stage, left, group):
        b, g = group // 4, group % 4
        part[stage, b, :, 256 * g : 256 * g + 256] = nt_dot(
            left, xg[256 * group : 256 * group + 256, :]
        ).astype(jnp.bfloat16)

    def scatter(stage, b):
        for k, (dx, dy) in enumerate(PEERS):
            px, py = peer(dx, dy)
            push(
                part.at[
                    stage,
                    b,
                    pl.ds(pl.multiple_of(16 * px, 16), 16),
                    pl.ds(pl.multiple_of(256 * py, 256), 256),
                ],
                sums_in.at[stage, b, k],
                rs_send.at[stage, b],
                rs_recv.at[stage, b],
                device(px, py, z, core),
            )

    def spread(stage, b):
        await_bytes(sums_in.at[stage, b], rs_recv.at[stage, b])
        rows = pl.ds(pl.multiple_of(16 * x, 16), 16)
        columns = pl.ds(pl.multiple_of(256 * y, 256), 256)
        acc = part[stage, b, rows, columns].astype(jnp.float32)
        for k in range(15):
            acc += sums_in[stage, b, k].astype(jnp.float32)
        wide[stage, b, rows, columns] = acc.astype(jnp.bfloat16)
        for dx, dy in PEERS:
            px, py = peer(dx, dy)
            push(
                wide.at[stage, b, rows, columns],
                wide.at[stage, b, rows, columns],
                ag_send.at[stage, b],
                ag_recv.at[stage, b],
                device(px, py, z, core),
            )

    def accumulate(stage, b):
        await_bytes(sums_in.at[stage, b], ag_recv.at[stage, b])
        product = nn_dot(wide[stage, b], xg[1024 * b : 1024 * b + 1024, :])
        if b == 0:
            total[stage] = product
        else:
            total[stage] += product

    for piece in range(PARTS):
        hand_on(0, (1, -1), piece)
    share(0)
    groups, spreads, sums = list(range(15)), [], []
    for far in ORDER:
        now = arrival(far)
        for piece in range(PARTS):
            for sign in signs(far):
                await_bytes(slot(far, sign, True, piece), ring_recv.at[piece, sem_at(far, sign)])
                hand_on(far, (sign,), piece)
        if far not in LEAVES:
            share(far)
        while groups and arrival(ORDER[groups[0]]) + 4.0 <= now:
            group = groups.pop(0)
            shared(ORDER[group])
            partial(0, tile[...], group)
            if group % 4 == 3:
                scatter(0, group // 4)
                spreads.append((now + 8.0, group // 4))
        while spreads and spreads[0][0] <= now:
            b = spreads.pop(0)[1]
            spread(0, b)
            sums.append((now + 8.0, b))
        while sums and sums[0][0] <= now:
            accumulate(0, sums.pop(0)[1])
    for group in groups + [15]:
        if group < 15:
            shared(ORDER[group])
        else:
            shared(STEPS)
            shared(0)
        partial(0, tile[...], group)
        if group % 4 == 3:
            scatter(0, group // 4)
            spreads.append((0.0, group // 4))
    for _, b in spreads[:-1]:
        spread(0, b)
        sums.append((0.0, b))
    for _, b in sums[:-1]:
        accumulate(0, b)
    spread(0, 3)
    accumulate(0, sums[-1][1])
    accumulate(0, 3)

    image = total[0].astype(jnp.bfloat16)
    for b in range(4):
        for g in range(4):
            partial(1, image, 4 * b + g)
        scatter(1, b)
    for b in range(4):
        spread(1, b)
    for b in range(4):
        accumulate(1, b)

    update = (output_gain * math.sqrt(max(M, D))) * (
        linear_weight * tile[...].astype(jnp.float32)
        + cubic_weight * image.astype(jnp.float32)
        + quintic_weight * total[1]
    )
    update = jnp.concatenate([update, jnp.zeros((ROWS, 128), jnp.float32)], axis=1)
    for j in range(4):
        block = update[:, 96 * j : 96 * j + 128].astype(jnp.bfloat16)
        for k in range(4):
            blocks[k, j] = block[16 * k : 16 * k + 16, :]

    landing = z_lo * 2 + core
    first_col = 16 * y + 4 * x

    def last_copy(k, j):
        return pltpu.make_async_remote_copy(
            src_ref=blocks.at[k, j],
            dst_ref=landed.at[landing],
            send_sem=last_send.at[4 * k + j],
            recv_sem=last_recv.at[landing],
            device_id=(4 * k + z_hi, first_col + j),
            device_id_type=MESH,
        )

    for k in range(4):
        for j in range(4):
            away = jnp.logical_or(x != k, col != first_col + j)

            @pl.when(away)
            def _(k=k, j=j):
                last_copy(k, j).start()

            @pl.when(jnp.logical_not(away))
            def _(k=k, j=j):
                pltpu.make_async_copy(
                    blocks.at[k, j], landed.at[landing], last_recv.at[landing]
                ).start()

    for k in range(16):
        await_bytes(landed.at[k], last_recv.at[k])
        block = landed[k].astype(jnp.float32)
        for j in range(4):
            out32[64 * j + 4 * k : 64 * j + 4 * k + 4, :] = block[4 * j : 4 * j + 4, :]
    out_ref[...] = out32[:, :96].astype(jnp.bfloat16)
    await_bytes(pieces.at[pl.ds(0, 15)], first_sem.at[0])
    for copy in sends:
        copy.wait_send()
    for stage in range(2):
        for b in range(4):
            await_bytes(sums_in.at[stage, b], rs_send.at[stage, b])
            await_bytes(sums_in.at[stage, b], ag_send.at[stage, b])
    for k in range(4):
        for j in range(4):

            @pl.when(jnp.logical_or(x != k, col != first_col + j))
            def _(k=k, j=j):
                last_copy(k, j).wait_send()


def shards(iterate):
    pieces = jnp.transpose(iterate.reshape(4, 16, WIDE), (1, 0, 2))
    spec = pl.BlockSpec(memory_space=pltpu.VMEM)
    return pl.pallas_call(
        kernel,
        out_shape=jax.ShapeDtypeStruct((256, 96), jnp.bfloat16),
        in_specs=[spec],
        out_specs=spec,
        scratch_shapes=[
            pltpu.VMEM((16, 4, WIDE), jnp.bfloat16),
            pltpu.VMEM((ROWS, WIDE), jnp.float32),
            pltpu.VMEM((M, WIDE), jnp.bfloat16),
            pltpu.VMEM((2, 4, ROWS, 1024), jnp.bfloat16),
            pltpu.VMEM((2, 4, 15, 16, 256), jnp.bfloat16),
            pltpu.VMEM((2, 4, ROWS, 1024), jnp.bfloat16),
            pltpu.VMEM((2, ROWS, WIDE), jnp.float32),
            pltpu.VMEM((4, 4, 16, 128), jnp.bfloat16),
            pltpu.VMEM((16, 16, 128), jnp.bfloat16),
            pltpu.VMEM((256, 128), jnp.float32),
            pltpu.SemaphoreType.DMA((2,)),
            pltpu.SemaphoreType.DMA((PARTS, 32)),
            pltpu.SemaphoreType.DMA((PARTS, 32)),
            pltpu.SemaphoreType.DMA((PARTS, 32)),
            pltpu.SemaphoreType.DMA((PARTS, 32)),
            pltpu.SemaphoreType.DMA((2, 4)),
            pltpu.SemaphoreType.DMA((2, 4)),
            pltpu.SemaphoreType.DMA((2, 4)),
            pltpu.SemaphoreType.DMA((2, 4)),
            pltpu.SemaphoreType.DMA((16,)),
            pltpu.SemaphoreType.DMA((16,)),
        ],
        compiler_params=pltpu.CompilerParams(collective_id=0, has_side_effects=True),
    )(pieces)


def solution(mesh):
    return jax.shard_map(
        shards,
        mesh=mesh,
        in_specs=(P(("row", "col"), None),),
        out_specs=P("row", "col"),
        check_vma=False,
    )
```
